32 devices in a mesh: section: 2 (over x), kvp: 16 (over z, y, core).
Axes of the slice: x: 2, y: 2, z: 4, core: 2. Of those that a mesh axis runs over, the one named last changes fastest.
Arguments:
- entering: bfloat16 [2, 8, 8192], P('section', None, 'kvp'), may hold values from -6 to 6
- newcomer: bfloat16 [1, 8, 8192], P(None, None, 'kvp'), may hold values from -6 to 6
- norm_gain: bfloat16 [2, 8192], P('section'), may hold values from 0.25 to 1.75
- query_weight: bfloat16 [2, 8192, 8192], P('section', None, 'kvp'), may hold values from -0.0625 to 0.0625
- keyvalue_weight: bfloat16 [2, 8192, 2048], P('section', None, 'kvp'), may hold values from -0.0625 to 0.0625
- key_cache: bfloat16 [2, 2, 8, 512, 1024], P('section', None, None, 'kvp'), may hold values from -96 to 96
- value_cache: bfloat16 [2, 2, 8, 512, 1024], P('section', None, None, 'kvp'), may hold values from -6 to 6
- cache_lengths: int32 [3, 8], replicated, may hold values from 1 to 512, as said below
Outputs:
- layer_outputs: bfloat16 [2, 2, 8, 8192], P('section', None, None, 'kvp')
The draws below stay inside these ranges and needn't reach their ends.
Inputs may be any that keep to these rules, and one draw needn't show every extreme that they name: `cache_lengths`: in every micro-batch some request has exactly 512 cached positions.
All inputs are finite; a program needn't handle non-finite values.
Results may differ from the reference program's by a relative error of at most 0.024.
The reference program's roundings to bfloat16 on the way count: a program that leaves them out, or rounds other values in their place, can miss the bound.
Values may be sent and summed in bfloat16 or wider, within the bound.
A program may use at most 128 MiB of HBM per device.

```python
import math
import jax
import jax.numpy as jnp
from jax import lax

D = 8192
NH = 64
KVH = 8
HD = 128
REQ = 8
TICKS = 2
CTX = 512
LAYERS = 2
MICRO = 3


def draw_key_cache(key, part):
    shape = (LAYERS, TICKS, REQ, CTX, KVH, HD)
    second_key = jax.random.fold_in(jax.random.fold_in(key, 11), 1)
    values = jnp.clip(jax.random.normal(second_key, shape, dtype=jnp.float32), -6.0, 6.0)
    return values.reshape(LAYERS, TICKS, REQ, CTX, KVH * HD).astype(jnp.bfloat16)


def draw_cache_lengths(key, part):
    first_key, second_key = jax.random.split(jax.random.fold_in(key, 23))
    drawn = jax.random.randint(first_key, (MICRO, REQ), 1, CTX + 1)
    chosen = jax.random.randint(second_key, (MICRO, 1), 0, REQ)
    longest = jnp.arange(REQ, dtype=jnp.int32)[None, :] == chosen
    return jnp.where(longest, CTX, drawn).astype(jnp.int32)


def shard_levels(key, shape, pieces, least, top_value):
    def one(dim, blocks):
        heights = jax.random.uniform(jax.random.fold_in(jax.random.fold_in(key, 6), dim), (blocks,), jnp.float32, least / len(pieces), top_value / len(pieces))
        return jnp.repeat(jnp.exp(heights), shape[dim] // blocks).reshape((-1,) + (1,) * (len(shape) - dim - 1))

    loudness = one(*pieces[0])
    for cut in pieces[1:]:
        loudness = loudness * one(*cut)
    return loudness


def gaussian(rng, dims, scale, most, pieces=(), kind=jnp.bfloat16):
    loudness = shard_levels(rng, dims, pieces, -0.22, 0.18) if pieces else 1.0
    entries = jax.random.normal(rng, dims, jnp.float32) * scale * loudness
    return jnp.minimum(jnp.maximum(entries, -most), most).astype(kind)


def setup_inputs(seed: int = 0) -> dict:
    streams_of = jax.random.split(jax.random.key(seed), 9)
    return {
        "entering": gaussian(streams_of[0], (LAYERS, REQ, D), 1.0, 6.0, ((0, 2), (2, 16))),
        "newcomer": gaussian(streams_of[1], (TICKS - 1, REQ, D), 1.0, 6.0, ((2, 16),)),
        "norm_gain": jnp.clip(1.0 + 0.15 * jax.random.normal(streams_of[2], (LAYERS, D), jnp.float32), 0.25, 1.75).astype(jnp.bfloat16),
        "query_weight": gaussian(streams_of[3], (LAYERS, D, NH * HD), D ** -0.5, 0.0625, ((0, 2), (2, 16))),
        "keyvalue_weight": gaussian(streams_of[4], (LAYERS, D, 2 * KVH * HD), D ** -0.5, 0.0625, ((0, 2), (2, 16))),
        "key_cache": draw_key_cache(jax.random.fold_in(streams_of[8], 71), 0),
        "value_cache": gaussian(streams_of[6], (LAYERS, TICKS, REQ, CTX, KVH * HD), 1.0, 6.0, ((0, 2), (3, 16))),
        "cache_lengths": draw_cache_lengths(jax.random.fold_in(streams_of[8], 71), 0),
    }


def rotate(values, positions):
    half_width = values.shape[-1] // 2
    exponent = jnp.arange(half_width, dtype=jnp.float32) * (2.0 / values.shape[-1])
    frequency = jnp.power(jnp.float32(500000.0), -exponent)
    angles = positions.astype(jnp.float32)[:, None, None] * frequency
    cosine = jnp.cos(angles)
    sine = jnp.sin(angles)
    first = values[..., :half_width]
    second = values[..., half_width:]
    return jnp.concatenate([first * cosine - second * sine, second * cosine + first * sine], axis=-1)

def section_layer(hidden, gain, query_w, keyvalue_w, cached_keys, cached_values, lengths_now):
    x_float = hidden.astype(jnp.float32)
    mean_square = lax.optimization_barrier(jnp.mean(x_float * x_float, axis=-1, keepdims=True))
    normed = (x_float * lax.rsqrt(mean_square + 1e-05) * gain.astype(jnp.float32)).astype(jnp.bfloat16)
    query = jnp.dot(normed, query_w, preferred_element_type=jnp.float32).reshape(REQ, NH, HD)
    query = rotate(query, lengths_now).astype(jnp.bfloat16)
    fresh = jnp.dot(normed, keyvalue_w, preferred_element_type=jnp.float32).astype(jnp.bfloat16)
    new_key = rotate(fresh[:, :KVH * HD].reshape(REQ, KVH, HD).astype(jnp.float32), lengths_now)
    new_value = fresh[:, KVH * HD:].reshape(REQ, KVH, HD).astype(jnp.float32)
    grouped = query.astype(jnp.float32).reshape(REQ, KVH, NH // KVH, HD)
    key_float = cached_keys.astype(jnp.float32).reshape(REQ, CTX, KVH, HD)
    value_float = cached_values.astype(jnp.float32).reshape(REQ, CTX, KVH, HD)
    score_scale = 1.0 / math.sqrt(HD)
    scores = jnp.einsum('bgrd,bpgd->bgrp', grouped, key_float) * score_scale
    in_cache = (jnp.arange(CTX, dtype=jnp.int32)[None, :] < lengths_now[:, None])[:, None, None, :]
    scores = jnp.where(in_cache, scores, jnp.float32(-1e+30))
    new_score = jnp.einsum('bgrd,bgd->bgr', grouped, new_key) * score_scale
    cache_max = lax.optimization_barrier(jnp.max(scores, axis=-1))
    top_score = jnp.maximum(cache_max, new_score)
    weights = jnp.where(in_cache, jnp.exp(scores - cache_max[..., None]), jnp.float32(0.0))
    value_weights = weights.astype(jnp.bfloat16).astype(jnp.float32)
    old_factor = jnp.exp(cache_max - top_score)
    new_weight = jnp.exp(new_score - top_score)
    denominator = lax.optimization_barrier(jnp.sum(weights, axis=-1)) * old_factor + new_weight
    weighted = jnp.einsum('bgrp,bpgd->bgrd', value_weights, value_float)
    numerator = weighted * old_factor[..., None] + new_weight[..., None] * new_value[:, :, None, :]
    attended = (numerator / denominator[..., None]).reshape(REQ, NH * HD)
    return (x_float + attended).astype(jnp.bfloat16)

def reference(entering, newcomer, norm_gain, query_weight, keyvalue_weight, key_cache, value_cache, cache_lengths):
    results = []
    for layer_index in range(LAYERS):
        results.append([None] * TICKS)
    for tick in range(TICKS):
        for layer_index in range(LAYERS):
            if tick == 0:
                hidden = entering[layer_index]
            elif layer_index == 0:
                hidden = newcomer[tick - 1]
            else:
                hidden = results[layer_index - 1][tick - 1]
            micro_id = tick + (LAYERS - 1 - layer_index)
            lengths_now = cache_lengths[micro_id]
            results[layer_index][tick] = section_layer(hidden, norm_gain[layer_index], query_weight[layer_index], keyvalue_weight[layer_index], key_cache[layer_index, tick], value_cache[layer_index, tick], lengths_now)
    return jnp.stack([jnp.stack(row, axis=0) for row in results], axis=0)
```

```python
import functools
import math

import jax
import jax.numpy as jnp
from jax import lax
from jax.experimental import pallas as pl
from jax.experimental.pallas import tpu as pltpu
from jax.sharding import PartitionSpec as P

NH = 64
KVH = 8
HD = 128
GROUP = NH // KVH
THETA = 500000.0
EPS = 1e-05
NEG = -1e30
MESH = pl.DeviceIdType.MESH
F32 = jnp.float32
BF16 = jnp.bfloat16


def three_parts(row):
    high = row.astype(BF16).astype(F32)
    rest = row - high
    middle = rest.astype(BF16).astype(F32)
    return [high, middle, rest - middle]


def layer_kernel(
    n,
    sections,
    lengths_ref,
    entering_ref,
    newcomer_ref,
    gain_hbm,
    query_hbm,
    keyvalue_hbm,
    keys_hbm,
    values_hbm,
    out_ref,
    query_w,
    keyvalue_w,
    keys,
    values,
    gain,
    inputs,
    normed,
    heads,
    staged,
    parts,
    leaving,
    columns,
    load_sem,
    weight_sem,
    cache_sem,
    send_sem,
    recv_sem,
):
    ticks, rows, width = out_ref.shape
    features = query_w.shape[0]
    own_heads = NH // n
    own_rows = own_heads * rows
    kv_width = keyvalue_w.shape[1]
    pieces = HD // kv_width
    group_rows = GROUP * rows
    span = keys.shape[1] // rows
    chunks = weight_sem.shape[0]
    depth = features // chunks
    scale = 1.0 / math.sqrt(HD)

    section = lax.axis_index("section")
    me = lax.axis_index("kvp")

    gain_load = pltpu.make_async_copy(gain_hbm, gain, load_sem.at[0])
    gain_load.start()
    own_loads = [
        pltpu.make_async_copy(entering_ref, inputs.at[0, me], load_sem.at[1])
    ]
    own_loads[0].start()
    weight_loads = []
    for c in range(chunks):
        part = pl.ds(c * depth, depth)
        weight_loads.append(
            (
                pltpu.make_async_copy(query_hbm.at[part], query_w.at[part], weight_sem.at[c, 0]),
                pltpu.make_async_copy(
                    keyvalue_hbm.at[part], keyvalue_w.at[part], weight_sem.at[c, 1]
                ),
            )
        )
        for load in weight_loads[-1]:
            load.start()
    cache_loads = []
    for t in range(ticks):
        cache_loads.append(
            (
                pltpu.make_async_copy(keys_hbm.at[t], keys.at[t], cache_sem.at[t, 0]),
                pltpu.make_async_copy(values_hbm.at[t], values.at[t], cache_sem.at[t, 1]),
            )
        )
        for load in cache_loads[-1]:
            load.start()

    def peer(step):
        return lax.rem(me + step, n)

    barrier = pltpu.get_barrier_semaphore()

    def greet(step, carry):
        pl.semaphore_signal(
            barrier, inc=1, device_id=(section, peer(step)), device_id_type=MESH
        )
        return carry

    lax.fori_loop(1, n, greet, 0)
    if sections > 1:

        @pl.when(section < sections - 1)
        def _():
            def greet_next(step, carry):
                pl.semaphore_signal(
                    barrier, inc=1, device_id=(section + 1, peer(step)), device_id_type=MESH
                )
                return carry

            lax.fori_loop(0, n, greet_next, 0)

        @pl.when(section > 0)
        def _():
            def greet_previous(step, carry):
                pl.semaphore_signal(
                    barrier, inc=1, device_id=(section - 1, peer(step)), device_id_type=MESH
                )
                return carry

            lax.fori_loop(0, n, greet_previous, 0)

    neighbours = (section > 0).astype(jnp.int32) + (section < sections - 1).astype(jnp.int32)
    pl.semaphore_wait(barrier, n - 1 + n * neighbours)

    def spread(source, target, tick, phase):
        def send(step, carry):
            pltpu.make_async_remote_copy(
                src_ref=source,
                dst_ref=target,
                send_sem=send_sem.at[tick, phase],
                recv_sem=recv_sem.at[tick, phase],
                device_id=(section, peer(step)),
                device_id_type=MESH,
            ).start()
            return carry

        lax.fori_loop(1, n, send, 0)

    def arrived(buffer, count, sem):
        whole = buffer.at[pl.ds(0, count)]
        pltpu.make_async_copy(whole, whole, sem).wait()

    spread(entering_ref, inputs.at[0, me], 0, 0)

    @pl.when(section == 0)
    def _():
        for t in range(1, ticks):
            pltpu.make_async_copy(
                newcomer_ref.at[t - 1], inputs.at[t, me], load_sem.at[1 + t]
            ).start()
            spread(newcomer_ref.at[t - 1], inputs.at[t, me], t, 0)

    lane = lax.broadcasted_iota(jnp.int32, (rows, HD), 1)
    row = lax.broadcasted_iota(jnp.int32, (rows, HD), 0)
    half = HD // 2
    exponent = (lane % half).astype(F32) * (2.0 / HD)
    frequency = jnp.exp(exponent * (-math.log(THETA)))
    turns = []
    masks = []
    place = lax.broadcasted_iota(jnp.int32, (rows * span, group_rows), 0)
    column = lax.broadcasted_iota(jnp.int32, (rows * span, group_rows), 1)
    position = me * span + place % span
    for t in range(ticks):
        micro = t + sections - 1 - section
        by_row = jnp.zeros((rows, HD), jnp.int32)
        limit = jnp.zeros((rows * span, group_rows), jnp.int32)
        for b in range(rows):
            length = lengths_ref[micro, b]
            by_row = jnp.where(row == b, length, by_row)
            limit = jnp.where(column % rows == b, length, limit)
        angles = by_row.astype(F32) * frequency
        sine = jnp.sin(angles)
        turns.append((jnp.cos(angles), jnp.where(lane < half, -sine, sine)))
        masks.append((place // span == column % rows) & (position < limit))

    def rotated(head, t):
        cosine, sine = turns[t]
        return head * cosine + pltpu.roll(head, half, 1) * sine

    gain_load.wait()
    for t in range(ticks):
        if t == 0:
            own_loads[0].wait()
            arrived(inputs.at[0], n - 1, recv_sem.at[0, 0])
        else:

            @pl.when(section == 0)
            def _():
                pltpu.make_async_copy(
                    newcomer_ref.at[t - 1], inputs.at[t, me], load_sem.at[1 + t]
                ).wait()
                arrived(inputs.at[t], n - 1, recv_sem.at[t, 0])

            @pl.when(section > 0)
            def _():
                arrived(inputs.at[t], n, recv_sem.at[t, 0])

        squares = jnp.zeros((rows, width), F32)
        for s in range(n):
            x = inputs[t, s].astype(F32)
            squares = squares + x * x
        mean_square = jnp.sum(squares, axis=-1, keepdims=True) * (1.0 / features)
        factor = lax.rsqrt(mean_square + EPS)
        for s in range(n):
            part = pl.ds(s * width, width)
            x = inputs[t, s].astype(F32)
            normed[:, part] = (x * factor * gain[:, part].astype(F32)).astype(BF16)

        query = jnp.zeros((rows, width), F32)
        fresh = jnp.zeros((rows, kv_width), F32)
        for c in range(chunks):
            part = pl.ds(c * depth, depth)
            if t == 0:
                for load in weight_loads[c]:
                    load.wait()
            query = query + jnp.dot(normed[:, part], query_w[part], preferred_element_type=F32)
            fresh = fresh + jnp.dot(normed[:, part], keyvalue_w[part], preferred_element_type=F32)
        message = [
            rotated(query[:, h * HD : (h + 1) * HD], t) for h in range(own_heads)
        ]
        fresh = fresh.astype(BF16).astype(F32)
        if pieces > 1:
            fresh = jnp.concatenate([fresh] * pieces, axis=1)
            fresh = jnp.where(lane // kv_width == me % pieces, fresh, 0.0)
        message.append(fresh)
        spare = heads.shape[2] - own_rows - rows
        if spare:
            message.append(jnp.zeros((spare, HD), F32))
        heads[t, me] = jnp.concatenate(message, axis=0).astype(BF16)
        spread(heads.at[t, me], heads.at[t, me], t, 1)

        for load in cache_loads[t]:
            load.wait()
        arrived(heads.at[t], n - 1, recv_sem.at[t, 1])
        valid = masks[t]
        per_group = GROUP // own_heads
        for g in range(KVH):
            grouped = jnp.concatenate(
                [
                    heads[t, g * per_group + j].astype(F32)[:own_rows]
                    for j in range(per_group)
                ],
                axis=0,
            ).astype(BF16)
            part = pl.ds(g * HD, HD)
            scores = lax.dot_general(
                keys[t, :, part],
                grouped,
                (((1,), (1,)), ((), ())),
                preferred_element_type=F32,
            )
            scores = jnp.where(valid, scores * scale, NEG)
            top = jnp.max(scores, axis=0, keepdims=True)
            weights = jnp.where(valid, jnp.exp(scores - top), 0.0)
            total = jnp.sum(weights, axis=0, keepdims=True)
            weighted = lax.dot_general(
                weights.astype(BF16),
                values[t, :, part],
                (((0,), (0,)), ((), ())),
                preferred_element_type=F32,
            )
            stats = jnp.concatenate(
                three_parts(top) + three_parts(total) + [jnp.zeros((2, group_rows), F32)], axis=0
            )
            stats = jnp.concatenate([stats, jnp.zeros((8, HD - group_rows), F32)], axis=1)
            for j in range(per_group):
                target = g * per_group + j
                message = [weighted[j * own_rows : (j + 1) * own_rows], stats]
                if spare:
                    message.append(jnp.zeros((spare, HD), F32))
                message = jnp.concatenate(message, axis=0).astype(BF16)
                staged[t, target] = message

                @pl.when(target == me)
                def _():
                    parts[t, me] = message

                @pl.when(target != me)
                def _():
                    pltpu.make_async_remote_copy(
                        src_ref=staged.at[t, target],
                        dst_ref=parts.at[t, me],
                        send_sem=send_sem.at[t, 2],
                        recv_sem=recv_sem.at[t, 2],
                        device_id=(section, target),
                        device_id_type=MESH,
                    ).start()

        group = (me * own_heads) // GROUP
        new_key = jnp.zeros((rows, HD), F32)
        new_value = jnp.zeros((rows, HD), F32)
        for j in range(pieces):
            new_key = new_key + heads[t, group * pieces + j].astype(F32)[own_rows : own_rows + rows]
            new_value = (
                new_value
                + heads[t, n // 2 + group * pieces + j].astype(F32)[own_rows : own_rows + rows]
            )
        new_key = jnp.concatenate([rotated(new_key, t)] * own_heads, axis=0)
        new_value = jnp.concatenate([new_value] * own_heads, axis=0)
        own_query = heads[t, me].astype(F32)[:own_rows]
        new_score = jnp.sum(own_query * new_key, axis=-1, keepdims=True) * scale

        arrived(parts.at[t], n - 1, recv_sem.at[t, 2])
        tops = []
        totals = []
        for s in range(n):
            stats = parts[t, s].astype(F32)[own_rows : own_rows + 8]
            tops.append(stats[0:1] + stats[1:2] + stats[2:3])
            totals.append(stats[3:4] + stats[4:5] + stats[5:6])
        blank = HD - n
        tops = jnp.concatenate(tops + [jnp.full((blank, HD), NEG, F32)], axis=0)
        totals = jnp.concatenate(totals + [jnp.zeros((blank, HD), F32)], axis=0)
        columns[0] = tops.T
        columns[1] = totals.T
        first = pl.multiple_of((me % per_group) * own_rows, 8)
        tops = columns[0, pl.ds(first, own_rows), :]
        totals = columns[1, pl.ds(first, own_rows), :]
        top = jnp.maximum(jnp.max(tops, axis=-1, keepdims=True), new_score)
        factors = jnp.exp(tops - top)
        new_weight = jnp.exp(new_score - top)
        denominator = jnp.sum(factors * totals, axis=-1, keepdims=True) + new_weight
        numerator = new_weight * new_value
        for s in range(n):
            part = parts[t, s].astype(F32)[:own_rows]
            numerator = numerator + part * factors[:, s : s + 1]
        attended = numerator / denominator
        attended = jnp.concatenate(
            [attended[h * rows : (h + 1) * rows] for h in range(own_heads)], axis=1
        )
        result = (inputs[t, me].astype(F32) + attended).astype(BF16)
        out_ref[t] = result
        if t < ticks - 1 and sections > 1:
            leaving[t] = result

            @pl.when(section < sections - 1)
            def _():
                def send(step, carry):
                    pltpu.make_async_remote_copy(
                        src_ref=leaving.at[t],
                        dst_ref=inputs.at[t + 1, me],
                        send_sem=send_sem.at[t, 3],
                        recv_sem=recv_sem.at[t + 1, 0],
                        device_id=(section + 1, peer(step)),
                        device_id_type=MESH,
                    ).start()
                    return carry

                lax.fori_loop(0, n, send, 0)

    for t in range(ticks):
        if t == 0:
            arrived(inputs.at[t], n - 1, send_sem.at[t, 0])
        else:

            @pl.when(section == 0)
            def _():
                arrived(inputs.at[t], n - 1, send_sem.at[t, 0])

        arrived(heads.at[t], n - 1, send_sem.at[t, 1])
        arrived(parts.at[t], n - 1, send_sem.at[t, 2])
        if t < ticks - 1 and sections > 1:

            @pl.when(section < sections - 1)
            def _():
                arrived(inputs.at[t], n, send_sem.at[t, 3])


def shards(
    n,
    sections,
    entering,
    newcomer,
    norm_gain,
    query_weight,
    keyvalue_weight,
    key_cache,
    value_cache,
    cache_lengths,
):
    _, rows, width = entering.shape
    _, features, _ = query_weight.shape
    kv_width = keyvalue_weight.shape[2]
    _, ticks, _, span, kv_features = key_cache.shape
    own_rows = (NH // n) * rows
    message_rows = -(-(own_rows + 8) // 16) * 16
    chunks = 4
    anywhere = pl.BlockSpec(memory_space=pl.ANY)
    out = pl.pallas_call(
        functools.partial(layer_kernel, n, sections),
        out_shape=jax.ShapeDtypeStruct((ticks, rows, width), BF16),
        in_specs=[pl.BlockSpec(memory_space=pltpu.SMEM)] + [anywhere] * 7,
        out_specs=pl.BlockSpec(memory_space=pltpu.VMEM),
        scratch_shapes=[
            pltpu.VMEM((features, width), BF16),
            pltpu.VMEM((features, kv_width), BF16),
            pltpu.VMEM((ticks, rows * span, kv_features), BF16),
            pltpu.VMEM((ticks, rows * span, kv_features), BF16),
            pltpu.VMEM((1, features), BF16),
            pltpu.VMEM((ticks, n, rows, width), BF16),
            pltpu.VMEM((rows, features), BF16),
            pltpu.VMEM((ticks, n, message_rows, HD), BF16),
            pltpu.VMEM((ticks, n, message_rows, HD), BF16),
            pltpu.VMEM((ticks, n, message_rows, HD), BF16),
            pltpu.VMEM((ticks, rows, width), BF16),
            pltpu.VMEM((2, HD, HD), F32),
            pltpu.SemaphoreType.DMA((1 + ticks,)),
            pltpu.SemaphoreType.DMA((chunks, 2)),
            pltpu.SemaphoreType.DMA((ticks, 2)),
            pltpu.SemaphoreType.DMA((ticks, 4)),
            pltpu.SemaphoreType.DMA((ticks, 3)),
        ],
        compiler_params=pltpu.CompilerParams(
            collective_id=0, has_side_effects=True, vmem_limit_bytes=40 << 20
        ),
    )(
        cache_lengths,
        entering[0],
        newcomer,
        norm_gain,
        query_weight[0],
        keyvalue_weight[0],
        key_cache.reshape(ticks, rows * span, kv_features),
        value_cache.reshape(ticks, rows * span, kv_features),
    )
    return out[None]


def solution(mesh):
    placed = (
        P("section", None, "kvp"),
        P(None, None, "kvp"),
        P("section", None),
        P("section", None, "kvp"),
        P("section", None, "kvp"),
        P("section", None, None, "kvp", None),
        P("section", None, None, "kvp", None),
        P(),
    )
    return jax.shard_map(
        functools.partial(shards, mesh.shape["kvp"], mesh.shape["section"]),
        mesh=mesh,
        in_specs=placed,
        out_specs=P("section", None, None, "kvp"),
        check_vma=False,
    )
```

```python
import functools
import math

import jax
import jax.numpy as jnp
from jax import lax
from jax.experimental import pallas as pl
from jax.experimental.pallas import tpu as pltpu
from jax.sharding import PartitionSpec as P

NH = 64
KVH = 8
HD = 128
GROUP = NH // KVH
THETA = 500000.0
EPS = 1e-05
NEG = -1e30
MESH = pl.DeviceIdType.MESH
F32 = jnp.float32
BF16 = jnp.bfloat16


def three_parts(row):
    high = row.astype(BF16).astype(F32)
    rest = row - high
    middle = rest.astype(BF16).astype(F32)
    return [high, middle, rest - middle]


def layer_kernel(
    n,
    sections,
    lengths_ref,
    entering_ref,
    newcomer_ref,
    gain_hbm,
    query_hbm,
    keyvalue_hbm,
    keys_hbm,
    values_hbm,
    out_ref,
    query_w,
    keyvalue_w,
    keys,
    values,
    gain,
    inputs,
    normed,
    heads,
    fresh_heads,
    staged,
    parts,
    leaving,
    columns,
    load_sem,
    weight_sem,
    cache_sem,
    send_sem,
    recv_sem,
    heads_sem,
    ready_sem,
):
    ticks, rows, width = out_ref.shape
    features = query_w.shape[0]
    own_heads = NH // n
    own_rows = own_heads * rows
    kv_width = keyvalue_w.shape[1]
    pieces = HD // kv_width
    group_rows = GROUP * rows
    span = keys.shape[1] // rows
    chunks = weight_sem.shape[0]
    depth = features // chunks
    scale = 1.0 / math.sqrt(HD)

    section = lax.axis_index("section")
    me = lax.axis_index("kvp")

    gain_load = pltpu.make_async_copy(gain_hbm, gain, load_sem.at[0])
    gain_load.start()
    own_loads = [
        pltpu.make_async_copy(entering_ref, inputs.at[0, me], load_sem.at[1])
    ]
    own_loads[0].start()
    weight_loads = []
    for c in range(chunks):
        part = pl.ds(c * depth, depth)
        weight_loads.append(
            (
                pltpu.make_async_copy(query_hbm.at[part], query_w.at[part], weight_sem.at[c, 0]),
                pltpu.make_async_copy(
                    keyvalue_hbm.at[part], keyvalue_w.at[part], weight_sem.at[c, 1]
                ),
            )
        )
        for load in weight_loads[-1]:
            load.start()
    cache_loads = []
    for t in range(ticks):
        cache_loads.append(
            (
                pltpu.make_async_copy(keys_hbm.at[t], keys.at[t], cache_sem.at[t, 0]),
                pltpu.make_async_copy(values_hbm.at[t], values.at[t], cache_sem.at[t, 1]),
            )
        )
        for load in cache_loads[-1]:
            load.start()

    per_group = GROUP // own_heads
    own_group = me // per_group

    def peer(step):
        group = lax.rem(own_group + step // per_group, KVH)
        return group * per_group + lax.rem(me + step, per_group)

    barrier = pltpu.get_barrier_semaphore()

    def greet(step, carry):
        pl.semaphore_signal(
            barrier, inc=1, device_id=(section, peer(step)), device_id_type=MESH
        )
        return carry

    lax.fori_loop(1, n, greet, 0)
    if sections > 1:

        @pl.when(section < sections - 1)
        def _():
            pl.semaphore_signal(barrier, inc=1, device_id=(section + 1, me), device_id_type=MESH)

        @pl.when(section > 0)
        def _():
            pl.semaphore_signal(barrier, inc=1, device_id=(section - 1, me), device_id_type=MESH)

    neighbours = (section > 0).astype(jnp.int32) + (section < sections - 1).astype(jnp.int32)
    pl.semaphore_wait(barrier, n - 1 + neighbours)
    if sections > 1:
        @pl.when(section > 0)
        def _():
            pl.semaphore_signal(ready_sem, inc=1, device_id=(section - 1, me), device_id_type=MESH)

    def spread(source, target, sent, received):
        def send(step, carry):
            pltpu.make_async_remote_copy(
                src_ref=source,
                dst_ref=target,
                send_sem=sent,
                recv_sem=received,
                device_id=(section, peer(step)),
                device_id_type=MESH,
            ).start()
            return carry

        lax.fori_loop(1, n, send, 0)

    def arrived(buffer, count, sem):
        whole = buffer.at[pl.ds(0, count)]
        pltpu.make_async_copy(whole, whole, sem).wait()

    spread(entering_ref, inputs.at[0, me], send_sem.at[0, 0], recv_sem.at[0, 0])

    @pl.when(section == 0)
    def _():
        for t in range(1, ticks):
            pltpu.make_async_copy(
                newcomer_ref.at[t - 1], inputs.at[t, me], load_sem.at[1 + t]
            ).start()
            spread(
                newcomer_ref.at[t - 1], inputs.at[t, me], send_sem.at[t, 0], recv_sem.at[t, 0]
            )

    lane = lax.broadcasted_iota(jnp.int32, (rows, HD), 1)
    row = lax.broadcasted_iota(jnp.int32, (rows, HD), 0)
    half = HD // 2
    exponent = (lane % half).astype(F32) * (2.0 / HD)
    frequency = jnp.exp(exponent * (-math.log(THETA)))
    turns = []
    masks = []
    place = lax.broadcasted_iota(jnp.int32, (rows * span, group_rows), 0)
    column = lax.broadcasted_iota(jnp.int32, (rows * span, group_rows), 1)
    position = me * span + place % span
    for t in range(ticks):
        micro = t + sections - 1 - section
        by_row = jnp.zeros((rows, HD), jnp.int32)
        limit = jnp.zeros((rows * span, group_rows), jnp.int32)
        for b in range(rows):
            length = lengths_ref[micro, b]
            by_row = jnp.where(row == b, length, by_row)
            limit = jnp.where(column % rows == b, length, limit)
        angles = by_row.astype(F32) * frequency
        sine = jnp.sin(angles)
        turns.append((jnp.cos(angles), jnp.where(lane < half, -sine, sine)))
        masks.append((place // span == column % rows) & (position < limit))

    def rotated(head, t):
        cosine, sine = turns[t]
        return head * cosine + pltpu.roll(head, half, 1) * sine

    kinds = n // 2
    fresh_group = (me % kinds) // pieces
    fresh_slot = (me // kinds) * pieces + me % pieces
    at_home = fresh_group == own_group

    def fresh_all(tick, sem, count):
        @pl.when(at_home)
        def _():
            if count > 1:
                arrived(fresh_heads.at[tick], count - 1, sem)

        @pl.when(jnp.logical_not(at_home))
        def _():
            arrived(fresh_heads.at[tick], count, sem)

    gain_load.wait()
    for t in range(ticks):
        if t == 0:
            own_loads[0].wait()
            arrived(inputs.at[0], n - 1, recv_sem.at[0, 0])
        else:

            @pl.when(section == 0)
            def _():
                pltpu.make_async_copy(
                    newcomer_ref.at[t - 1], inputs.at[t, me], load_sem.at[1 + t]
                ).wait()
                arrived(inputs.at[t], n - 1, recv_sem.at[t, 0])

            @pl.when(section > 0)
            def _():
                arrived(inputs.at[t], n, recv_sem.at[t, 0])

        squares = jnp.zeros((rows, width), F32)
        for s in range(n):
            x = inputs[t, s].astype(F32)
            squares = squares + x * x
        mean_square = jnp.sum(squares, axis=-1, keepdims=True) * (1.0 / features)
        factor = lax.rsqrt(mean_square + EPS)
        for s in range(n):
            part = pl.ds(s * width, width)
            x = inputs[t, s].astype(F32)
            normed[:, part] = (x * factor * gain[:, part].astype(F32)).astype(BF16)

        query = jnp.zeros((rows, width), F32)
        fresh = jnp.zeros((rows, kv_width), F32)
        for c in range(chunks):
            part = pl.ds(c * depth, depth)
            if t == 0:
                for load in weight_loads[c]:
                    load.wait()
            query = query + jnp.dot(normed[:, part], query_w[part], preferred_element_type=F32)
            fresh = fresh + jnp.dot(normed[:, part], keyvalue_w[part], preferred_element_type=F32)
        heads[t, me] = jnp.concatenate(
            [rotated(query[:, h * HD : (h + 1) * HD], t) for h in range(own_heads)], axis=0
        ).astype(BF16)
        spread(heads.at[t, me], heads.at[t, me], send_sem.at[t, 1], heads_sem.at[t, own_group])
        fresh = fresh.astype(BF16)
        if pieces > 1:
            fresh = jnp.concatenate([fresh.astype(F32)] * pieces, axis=1)
            fresh = jnp.where(lane // kv_width == me % pieces, fresh, 0.0).astype(BF16)
        fresh_heads[t, 2 * pieces] = fresh
        for j in range(per_group):
            target = fresh_group * per_group + j

            @pl.when(target == me)
            def _():
                fresh_heads[t, fresh_slot] = fresh

            @pl.when(target != me)
            def _():
                pltpu.make_async_remote_copy(
                    src_ref=fresh_heads.at[t, 2 * pieces],
                    dst_ref=fresh_heads.at[t, fresh_slot],
                    send_sem=send_sem.at[t, 4],
                    recv_sem=recv_sem.at[t, 1],
                    device_id=(section, target),
                    device_id_type=MESH,
                ).start()

        for load in cache_loads[t]:
            load.wait()
        valid = masks[t]
        for k in range(KVH):
            g = lax.rem(own_group + KVH - k, KVH)
            if k > 0 or per_group > 1:
                arrived(heads.at[t], per_group - (k == 0), heads_sem.at[t, g])
            grouped = jnp.concatenate(
                [heads[t, g * per_group + j].astype(F32) for j in range(per_group)], axis=0
            ).astype(BF16)
            part = pl.ds(pl.multiple_of(g * HD, HD), HD)
            scores = lax.dot_general(
                keys[t, :, part],
                grouped,
                (((1,), (1,)), ((), ())),
                preferred_element_type=F32,
            )
            scores = jnp.where(valid, scores * scale, NEG)
            top = jnp.max(scores, axis=0, keepdims=True)
            weights = jnp.where(valid, jnp.exp(scores - top), 0.0)
            total = jnp.sum(weights, axis=0, keepdims=True)
            weighted = lax.dot_general(
                weights.astype(BF16),
                values[t, :, part],
                (((0,), (0,)), ((), ())),
                preferred_element_type=F32,
            )
            stats = jnp.concatenate(
                three_parts(top) + three_parts(total) + [jnp.zeros((2, group_rows), F32)], axis=0
            )
            stats = jnp.concatenate([stats, jnp.zeros((8, HD - group_rows), F32)], axis=1)
            for j in range(per_group):
                target = g * per_group + j
                message = jnp.concatenate(
                    [weighted[j * own_rows : (j + 1) * own_rows], stats], axis=0
                ).astype(BF16)
                staged[t, target] = message

                def send():
                    pltpu.make_async_remote_copy(
                        src_ref=staged.at[t, target],
                        dst_ref=parts.at[t, me],
                        send_sem=send_sem.at[t, 2],
                        recv_sem=recv_sem.at[t, 2],
                        device_id=(section, target),
                        device_id_type=MESH,
                    ).start()

                if k > 0:
                    send()
                else:

                    @pl.when(target == me)
                    def _():
                        parts[t, me] = message

                    pl.when(target != me)(send)

        fresh_all(t, recv_sem.at[t, 1], 2 * pieces)
        new_key = jnp.zeros((rows, HD), F32)
        new_value = jnp.zeros((rows, HD), F32)
        for j in range(pieces):
            new_key = new_key + fresh_heads[t, j].astype(F32)
            new_value = new_value + fresh_heads[t, pieces + j].astype(F32)
        new_key = jnp.concatenate([rotated(new_key, t)] * own_heads, axis=0)
        new_value = jnp.concatenate([new_value] * own_heads, axis=0)
        own_query = heads[t, me].astype(F32)
        new_score = jnp.sum(own_query * new_key, axis=-1, keepdims=True) * scale

        arrived(parts.at[t], n - 1, recv_sem.at[t, 2])
        tops = []
        totals = []
        for s in range(n):
            stats = parts[t, s].astype(F32)[own_rows : own_rows + 8]
            tops.append(stats[0:1] + stats[1:2] + stats[2:3])
            totals.append(stats[3:4] + stats[4:5] + stats[5:6])
        blank = HD - n
        tops = jnp.concatenate(tops + [jnp.full((blank, HD), NEG, F32)], axis=0)
        totals = jnp.concatenate(totals + [jnp.zeros((blank, HD), F32)], axis=0)
        columns[0] = tops.T
        columns[1] = totals.T
        first = pl.multiple_of((me % per_group) * own_rows, 8)
        tops = columns[0, pl.ds(first, own_rows), :]
        totals = columns[1, pl.ds(first, own_rows), :]
        top = jnp.maximum(jnp.max(tops, axis=-1, keepdims=True), new_score)
        factors = jnp.exp(tops - top)
        new_weight = jnp.exp(new_score - top)
        denominator = jnp.sum(factors * totals, axis=-1, keepdims=True) + new_weight
        numerator = new_weight * new_value
        for s in range(n):
            part = parts[t, s].astype(F32)[:own_rows]
            numerator = numerator + part * factors[:, s : s + 1]
        attended = numerator / denominator
        attended = jnp.concatenate(
            [attended[h * rows : (h + 1) * rows] for h in range(own_heads)], axis=1
        )
        result = (inputs[t, me].astype(F32) + attended).astype(BF16)
        out_ref[t] = result
        if t < ticks - 1 and sections > 1:
            leaving[t] = result

            @pl.when(section < sections - 1)
            def _():
                if t == 0:
                    pl.semaphore_wait(ready_sem, 1)

                def send(step, carry):
                    pltpu.make_async_remote_copy(
                        src_ref=leaving.at[t],
                        dst_ref=inputs.at[t + 1, me],
                        send_sem=send_sem.at[t, 3],
                        recv_sem=recv_sem.at[t + 1, 0],
                        device_id=(section + 1, peer(step)),
                        device_id_type=MESH,
                    ).start()
                    return carry

                lax.fori_loop(0, n, send, 0)

    for t in range(ticks):
        if t == 0:
            arrived(inputs.at[t], n - 1, send_sem.at[t, 0])
        else:

            @pl.when(section == 0)
            def _():
                arrived(inputs.at[t], n - 1, send_sem.at[t, 0])

        arrived(heads.at[t], n - 1, send_sem.at[t, 1])
        fresh_all(t, send_sem.at[t, 4], per_group)
        arrived(parts.at[t], n - 1, send_sem.at[t, 2])
        if t < ticks - 1 and sections > 1:

            @pl.when(section < sections - 1)
            def _():
                arrived(inputs.at[t], n, send_sem.at[t, 3])


def shards(
    n,
    sections,
    entering,
    newcomer,
    norm_gain,
    query_weight,
    keyvalue_weight,
    key_cache,
    value_cache,
    cache_lengths,
):
    _, rows, width = entering.shape
    _, features, _ = query_weight.shape
    kv_width = keyvalue_weight.shape[2]
    _, ticks, _, span, kv_features = key_cache.shape
    own_rows = (NH // n) * rows
    message_rows = own_rows + 8
    pieces = HD // kv_width
    slots = max(2 * pieces + 1, NH // KVH * n // NH)
    chunks = 4
    anywhere = pl.BlockSpec(memory_space=pl.ANY)
    out = pl.pallas_call(
        functools.partial(layer_kernel, n, sections),
        out_shape=jax.ShapeDtypeStruct((ticks, rows, width), BF16),
        in_specs=[pl.BlockSpec(memory_space=pltpu.SMEM)] + [anywhere] * 7,
        out_specs=pl.BlockSpec(memory_space=pltpu.VMEM),
        scratch_shapes=[
            pltpu.VMEM((features, width), BF16),
            pltpu.VMEM((features, kv_width), BF16),
            pltpu.VMEM((ticks, rows * span, kv_features), BF16),
            pltpu.VMEM((ticks, rows * span, kv_features), BF16),
            pltpu.VMEM((1, features), BF16),
            pltpu.VMEM((ticks, n, rows, width), BF16),
            pltpu.VMEM((rows, features), BF16),
            pltpu.VMEM((ticks, n, own_rows, HD), BF16),
            pltpu.VMEM((ticks, slots, rows, HD), BF16),
            pltpu.VMEM((ticks, n, message_rows, HD), BF16),
            pltpu.VMEM((ticks, n, message_rows, HD), BF16),
            pltpu.VMEM((ticks, rows, width), BF16),
            pltpu.VMEM((2, HD, HD), F32),
            pltpu.SemaphoreType.DMA((1 + ticks,)),
            pltpu.SemaphoreType.DMA((chunks, 2)),
            pltpu.SemaphoreType.DMA((ticks, 2)),
            pltpu.SemaphoreType.DMA((ticks, 5)),
            pltpu.SemaphoreType.DMA((ticks, 3)),
            pltpu.SemaphoreType.DMA((ticks, KVH)),
            pltpu.SemaphoreType.REGULAR,
        ],
        compiler_params=pltpu.CompilerParams(
            collective_id=0, has_side_effects=True, vmem_limit_bytes=60 << 20
        ),
    )(
        cache_lengths,
        entering[0],
        newcomer,
        norm_gain,
        query_weight[0],
        keyvalue_weight[0],
        key_cache.reshape(ticks, rows * span, kv_features),
        value_cache.reshape(ticks, rows * span, kv_features),
    )
    return out[None]


def solution(mesh):
    placed = (
        P("section", None, "kvp"),
        P(None, None, "kvp"),
        P("section", None),
        P("section", None, "kvp"),
        P("section", None, "kvp"),
        P("section", None, None, "kvp", None),
        P("section", None, None, "kvp", None),
        P(),
    )
    return jax.shard_map(
        functools.partial(shards, mesh.shape["kvp"], mesh.shape["section"]),
        mesh=mesh,
        in_specs=placed,
        out_specs=P("section", None, None, "kvp"),
        check_vma=False,
    )
```

```python
import functools
import math

import jax
import jax.numpy as jnp
from jax import lax
from jax.experimental import pallas as pl
from jax.experimental.pallas import tpu as pltpu
from jax.sharding import PartitionSpec as P

NH = 64
KVH = 8
HD = 128
GROUP = NH // KVH
PAIRS = KVH // 2
THETA = 500000.0
EPS = 1e-05
NEG = -1e30
MESH = pl.DeviceIdType.MESH
F32 = jnp.float32
BF16 = jnp.bfloat16


def three_parts(row):
    high = row.astype(BF16).astype(F32)
    rest = row - high
    middle = rest.astype(BF16).astype(F32)
    return [high, middle, rest - middle]


def layer_kernel(
    n,
    sections,
    lengths_ref,
    entering_ref,
    newcomer_ref,
    gain_hbm,
    query_hbm,
    keyvalue_hbm,
    keys_hbm,
    values_hbm,
    out_ref,
    query_w,
    keyvalue_w,
    keys,
    values,
    gain,
    inputs,
    normed,
    heads,
    fresh_heads,
    staged,
    parts,
    leaving,
    columns,
    load_sem,
    weight_sem,
    cache_sem,
    send_sem,
    recv_sem,
    heads_sem,
    ready_sem,
):
    ticks, rows, width = out_ref.shape
    features = query_w.shape[0]
    own_heads = NH // n
    own_rows = own_heads * rows
    kv_width = keyvalue_w.shape[1]
    pieces = HD // kv_width
    group_rows = GROUP * rows
    pair_rows = 2 * group_rows
    span = keys.shape[1] // rows
    chunks = weight_sem.shape[0]
    depth = features // chunks
    scale = 1.0 / math.sqrt(HD)

    section = lax.axis_index("section")
    me = lax.axis_index("kvp")

    gain_load = pltpu.make_async_copy(gain_hbm, gain, load_sem.at[0])
    gain_load.start()
    own_loads = [
        pltpu.make_async_copy(entering_ref, inputs.at[0, me], load_sem.at[1])
    ]
    own_loads[0].start()
    weight_loads = []
    for c in range(chunks):
        part = pl.ds(c * depth, depth)
        weight_loads.append(
            (
                pltpu.make_async_copy(query_hbm.at[part], query_w.at[part], weight_sem.at[c, 0]),
                pltpu.make_async_copy(
                    keyvalue_hbm.at[part], keyvalue_w.at[part], weight_sem.at[c, 1]
                ),
            )
        )
        for load in weight_loads[-1]:
            load.start()
    cache_loads = []
    for t in range(ticks):
        cache_loads.append(
            (
                pltpu.make_async_copy(keys_hbm.at[t], keys.at[t], cache_sem.at[t, 0]),
                pltpu.make_async_copy(values_hbm.at[t], values.at[t], cache_sem.at[t, 1]),
            )
        )
        for load in cache_loads[-1]:
            load.start()

    per_group = GROUP // own_heads
    own_group = me // per_group

    per_pair = 2 * per_group
    own_pair = me // per_pair

    def peer(step):
        pair = lax.rem(own_pair + step // per_pair, PAIRS)
        return pair * per_pair + lax.rem(me + step, per_pair)

    barrier = pltpu.get_barrier_semaphore()

    def greet(step, carry):
        pl.semaphore_signal(
            barrier, inc=1, device_id=(section, peer(step)), device_id_type=MESH
        )
        return carry

    lax.fori_loop(1, n, greet, 0)
    if sections > 1:

        @pl.when(section < sections - 1)
        def _():
            pl.semaphore_signal(barrier, inc=1, device_id=(section + 1, me), device_id_type=MESH)

        @pl.when(section > 0)
        def _():
            pl.semaphore_signal(barrier, inc=1, device_id=(section - 1, me), device_id_type=MESH)

    neighbours = (section > 0).astype(jnp.int32) + (section < sections - 1).astype(jnp.int32)
    pl.semaphore_wait(barrier, n - 1 + neighbours)
    if sections > 1:
        @pl.when(section > 0)
        def _():
            pl.semaphore_signal(ready_sem, inc=1, device_id=(section - 1, me), device_id_type=MESH)

    def spread(source, target, sent, received):
        def send(step, carry):
            pltpu.make_async_remote_copy(
                src_ref=source,
                dst_ref=target,
                send_sem=sent,
                recv_sem=received,
                device_id=(section, peer(step)),
                device_id_type=MESH,
            ).start()
            return carry

        lax.fori_loop(1, n, send, 0)

    def arrived(buffer, count, sem):
        whole = buffer.at[pl.ds(0, count)]
        pltpu.make_async_copy(whole, whole, sem).wait()

    spread(entering_ref, inputs.at[0, me], send_sem.at[0, 0], recv_sem.at[0, 0])

    @pl.when(section == 0)
    def _():
        for t in range(1, ticks):
            pltpu.make_async_copy(
                newcomer_ref.at[t - 1], inputs.at[t, me], load_sem.at[1 + t]
            ).start()
            spread(
                newcomer_ref.at[t - 1], inputs.at[t, me], send_sem.at[t, 0], recv_sem.at[t, 0]
            )

    lane = lax.broadcasted_iota(jnp.int32, (rows, HD), 1)
    row = lax.broadcasted_iota(jnp.int32, (rows, HD), 0)
    half = HD // 2
    exponent = (lane % half).astype(F32) * (2.0 / HD)
    frequency = jnp.exp(exponent * (-math.log(THETA)))
    turns = []
    masks = []
    place = lax.broadcasted_iota(jnp.int32, (rows * span, pair_rows), 0)
    column = lax.broadcasted_iota(jnp.int32, (rows * span, pair_rows), 1)
    position = me * span + place % span
    for t in range(ticks):
        micro = t + sections - 1 - section
        by_row = jnp.zeros((rows, HD), jnp.int32)
        limit = jnp.zeros((rows * span, pair_rows), jnp.int32)
        for b in range(rows):
            length = lengths_ref[micro, b]
            by_row = jnp.where(row == b, length, by_row)
            limit = jnp.where(column % rows == b, length, limit)
        angles = by_row.astype(F32) * frequency
        sine = jnp.sin(angles)
        turns.append((jnp.cos(angles), jnp.where(lane < half, -sine, sine)))
        masks.append((place // span == column % rows) & (position < limit))

    def rotated(head, t):
        cosine, sine = turns[t]
        return head * cosine + pltpu.roll(head, half, 1) * sine

    kinds = n // 2
    fresh_group = (me % kinds) // pieces
    fresh_slot = (me // kinds) * pieces + me % pieces
    at_home = fresh_group == own_group

    def fresh_all(tick, sem, count):
        @pl.when(at_home)
        def _():
            if count > 1:
                arrived(fresh_heads.at[tick], count - 1, sem)

        @pl.when(jnp.logical_not(at_home))
        def _():
            arrived(fresh_heads.at[tick], count, sem)

    gain_load.wait()
    for t in range(ticks):
        if t == 0:
            own_loads[0].wait()
            arrived(inputs.at[0], n - 1, recv_sem.at[0, 0])
        else:

            @pl.when(section == 0)
            def _():
                pltpu.make_async_copy(
                    newcomer_ref.at[t - 1], inputs.at[t, me], load_sem.at[1 + t]
                ).wait()
                arrived(inputs.at[t], n - 1, recv_sem.at[t, 0])

            @pl.when(section > 0)
            def _():
                arrived(inputs.at[t], n, recv_sem.at[t, 0])

        squares = jnp.zeros((rows, width), F32)
        for s in range(n):
            x = inputs[t, s].astype(F32)
            squares = squares + x * x
        mean_square = jnp.sum(squares, axis=-1, keepdims=True) * (1.0 / features)
        factor = lax.rsqrt(mean_square + EPS)
        for s in range(n):
            part = pl.ds(s * width, width)
            x = inputs[t, s].astype(F32)
            normed[:, part] = (x * factor * gain[:, part].astype(F32)).astype(BF16)

        query = jnp.zeros((rows, width), F32)
        for c in range(chunks):
            part = pl.ds(c * depth, depth)
            if t == 0:
                weight_loads[c][0].wait()
            query = query + jnp.dot(normed[:, part], query_w[part], preferred_element_type=F32)
        heads[t, me] = jnp.concatenate(
            [rotated(query[:, h * HD : (h + 1) * HD], t) for h in range(own_heads)], axis=0
        ).astype(BF16)
        spread(heads.at[t, me], heads.at[t, me], send_sem.at[t, 1], heads_sem.at[t, own_pair])
        fresh = jnp.zeros((rows, kv_width), F32)
        for c in range(chunks):
            part = pl.ds(c * depth, depth)
            if t == 0:
                weight_loads[c][1].wait()
            fresh = fresh + jnp.dot(normed[:, part], keyvalue_w[part], preferred_element_type=F32)
        fresh = fresh.astype(BF16)
        if pieces > 1:
            fresh = jnp.concatenate([fresh.astype(F32)] * pieces, axis=1)
            fresh = jnp.where(lane // kv_width == me % pieces, fresh, 0.0).astype(BF16)
        fresh_heads[t, 2 * pieces] = fresh
        for j in range(per_group):
            target = fresh_group * per_group + j

            @pl.when(target == me)
            def _():
                fresh_heads[t, fresh_slot] = fresh

            @pl.when(target != me)
            def _():
                pltpu.make_async_remote_copy(
                    src_ref=fresh_heads.at[t, 2 * pieces],
                    dst_ref=fresh_heads.at[t, fresh_slot],
                    send_sem=send_sem.at[t, 4],
                    recv_sem=recv_sem.at[t, 1],
                    device_id=(section, target),
                    device_id_type=MESH,
                ).start()

        for load in cache_loads[t]:
            load.wait()
        valid = masks[t]
        upper = lax.broadcasted_iota(jnp.int32, (pair_rows, HD), 0) < group_rows
        for k in range(PAIRS):
            pair = lax.rem(own_pair + PAIRS - k, PAIRS)
            arrived(heads.at[t], per_pair - (k == 0), heads_sem.at[t, pair])
            both = jnp.concatenate(
                [heads[t, pair * per_pair + j].astype(F32) for j in range(per_pair)], axis=0
            )
            both = jnp.concatenate(
                [jnp.where(upper, both, 0.0), jnp.where(upper, 0.0, both)], axis=1
            ).astype(BF16)
            part = pl.ds(pl.multiple_of(pair * 2 * HD, 2 * HD), 2 * HD)
            scores = lax.dot_general(
                keys[t, :, part],
                both,
                (((1,), (1,)), ((), ())),
                preferred_element_type=F32,
            )
            scores = jnp.where(valid, scores * scale, NEG)
            top = jnp.max(scores, axis=0, keepdims=True)
            weights = jnp.where(valid, jnp.exp(scores - top), 0.0)
            total = jnp.sum(weights, axis=0, keepdims=True)
            weighted = lax.dot_general(
                weights.astype(BF16),
                values[t, :, part],
                (((0,), (0,)), ((), ())),
                preferred_element_type=F32,
            )
            weighted = jnp.where(upper, weighted[:, :HD], weighted[:, HD:])
            stats = jnp.concatenate(
                three_parts(top) + three_parts(total) + [jnp.zeros((2, pair_rows), F32)], axis=0
            )
            for j in range(per_pair):
                target = pair * per_pair + j
                message = jnp.concatenate(
                    [weighted[j * own_rows : (j + 1) * own_rows], stats], axis=0
                ).astype(BF16)
                staged[t, target] = message

                def send():
                    pltpu.make_async_remote_copy(
                        src_ref=staged.at[t, target],
                        dst_ref=parts.at[t, me],
                        send_sem=send_sem.at[t, 2],
                        recv_sem=recv_sem.at[t, 2],
                        device_id=(section, target),
                        device_id_type=MESH,
                    ).start()

                if k > 0:
                    send()
                else:

                    @pl.when(target == me)
                    def _():
                        parts[t, me] = message

                    pl.when(target != me)(send)

        fresh_all(t, recv_sem.at[t, 1], 2 * pieces)
        new_key = jnp.zeros((rows, HD), F32)
        new_value = jnp.zeros((rows, HD), F32)
        for j in range(pieces):
            new_key = new_key + fresh_heads[t, j].astype(F32)
            new_value = new_value + fresh_heads[t, pieces + j].astype(F32)
        new_key = jnp.concatenate([rotated(new_key, t)] * own_heads, axis=0)
        new_value = jnp.concatenate([new_value] * own_heads, axis=0)
        own_query = heads[t, me].astype(F32)
        new_score = jnp.sum(own_query * new_key, axis=-1, keepdims=True) * scale

        arrived(parts.at[t], n - 1, recv_sem.at[t, 2])
        tops = []
        totals = []
        for s in range(n):
            stats = parts[t, s].astype(F32)[own_rows : own_rows + 8]
            tops.append(stats[0:1] + stats[1:2] + stats[2:3])
            totals.append(stats[3:4] + stats[4:5] + stats[5:6])
        blank = HD - n
        tops = jnp.concatenate(tops + [jnp.full((blank, HD), NEG, F32)], axis=0)
        totals = jnp.concatenate(totals + [jnp.zeros((blank, HD), F32)], axis=0)
        columns[0] = tops.T
        columns[1] = totals.T
        first = pl.multiple_of((me % per_pair) * own_rows, 8)
        tops = columns[0, pl.ds(first, own_rows), :]
        totals = columns[1, pl.ds(first, own_rows), :]
        top = jnp.maximum(jnp.max(tops, axis=-1, keepdims=True), new_score)
        factors = jnp.exp(tops - top)
        new_weight = jnp.exp(new_score - top)
        denominator = jnp.sum(factors * totals, axis=-1, keepdims=True) + new_weight
        numerator = new_weight * new_value
        for s in range(n):
            part = parts[t, s].astype(F32)[:own_rows]
            numerator = numerator + part * factors[:, s : s + 1]
        attended = numerator / denominator
        attended = jnp.concatenate(
            [attended[h * rows : (h + 1) * rows] for h in range(own_heads)], axis=1
        )
        result = (inputs[t, me].astype(F32) + attended).astype(BF16)
        out_ref[t] = result
        if t < ticks - 1 and sections > 1:
            leaving[t] = result

            @pl.when(section < sections - 1)
            def _():
                if t == 0:
                    pl.semaphore_wait(ready_sem, 1)

                def send(step, carry):
                    pltpu.make_async_remote_copy(
                        src_ref=leaving.at[t],
                        dst_ref=inputs.at[t + 1, me],
                        send_sem=send_sem.at[t, 3],
                        recv_sem=recv_sem.at[t + 1, 0],
                        device_id=(section + 1, peer(step)),
                        device_id_type=MESH,
                    ).start()
                    return carry

                lax.fori_loop(0, n, send, 0)

    for t in range(ticks):
        if t == 0:
            arrived(inputs.at[t], n - 1, send_sem.at[t, 0])
        else:

            @pl.when(section == 0)
            def _():
                arrived(inputs.at[t], n - 1, send_sem.at[t, 0])

        arrived(heads.at[t], n - 1, send_sem.at[t, 1])
        fresh_all(t, send_sem.at[t, 4], per_group)
        arrived(parts.at[t], n - 1, send_sem.at[t, 2])
        if t < ticks - 1 and sections > 1:

            @pl.when(section < sections - 1)
            def _():
                arrived(inputs.at[t], n, send_sem.at[t, 3])


def shards(
    n,
    sections,
    entering,
    newcomer,
    norm_gain,
    query_weight,
    keyvalue_weight,
    key_cache,
    value_cache,
    cache_lengths,
):
    _, rows, width = entering.shape
    _, features, _ = query_weight.shape
    kv_width = keyvalue_weight.shape[2]
    _, ticks, _, span, kv_features = key_cache.shape
    own_rows = (NH // n) * rows
    message_rows = own_rows + 8
    pieces = HD // kv_width
    slots = max(2 * pieces + 1, NH // KVH * n // NH)
    chunks = 4
    anywhere = pl.BlockSpec(memory_space=pl.ANY)
    out = pl.pallas_call(
        functools.partial(layer_kernel, n, sections),
        out_shape=jax.ShapeDtypeStruct((ticks, rows, width), BF16),
        in_specs=[pl.BlockSpec(memory_space=pltpu.SMEM)] + [anywhere] * 7,
        out_specs=pl.BlockSpec(memory_space=pltpu.VMEM),
        scratch_shapes=[
            pltpu.VMEM((features, width), BF16),
            pltpu.VMEM((features, kv_width), BF16),
            pltpu.VMEM((ticks, rows * span, kv_features), BF16),
            pltpu.VMEM((ticks, rows * span, kv_features), BF16),
            pltpu.VMEM((1, features), BF16),
            pltpu.VMEM((ticks, n, rows, width), BF16),
            pltpu.VMEM((rows, features), BF16),
            pltpu.VMEM((ticks, n, own_rows, HD), BF16),
            pltpu.VMEM((ticks, slots, rows, HD), BF16),
            pltpu.VMEM((ticks, n, message_rows, HD), BF16),
            pltpu.VMEM((ticks, n, message_rows, HD), BF16),
            pltpu.VMEM((ticks, rows, width), BF16),
            pltpu.VMEM((2, HD, HD), F32),
            pltpu.SemaphoreType.DMA((1 + ticks,)),
            pltpu.SemaphoreType.DMA((chunks, 2)),
            pltpu.SemaphoreType.DMA((ticks, 2)),
            pltpu.SemaphoreType.DMA((ticks, 5)),
            pltpu.SemaphoreType.DMA((ticks, 3)),
            pltpu.SemaphoreType.DMA((ticks, PAIRS)),
            pltpu.SemaphoreType.REGULAR,
        ],
        compiler_params=pltpu.CompilerParams(
            collective_id=0, has_side_effects=True, vmem_limit_bytes=60 << 20
        ),
    )(
        cache_lengths,
        entering[0],
        newcomer,
        norm_gain,
        query_weight[0],
        keyvalue_weight[0],
        key_cache.reshape(ticks, rows * span, kv_features),
        value_cache.reshape(ticks, rows * span, kv_features),
    )
    return out[None]


def solution(mesh):
    placed = (
        P("section", None, "kvp"),
        P(None, None, "kvp"),
        P("section", None),
        P("section", None, "kvp"),
        P("section", None, "kvp"),
        P("section", None, None, "kvp", None),
        P("section", None, None, "kvp", None),
        P(),
    )
    return jax.shard_map(
        functools.partial(shards, mesh.shape["kvp"], mesh.shape["section"]),
        mesh=mesh,
        in_specs=placed,
        out_specs=P("section", None, None, "kvp"),
        check_vma=False,
    )
```

```python
import functools
import math

import jax
import jax.numpy as jnp
from jax import lax
from jax.experimental import pallas as pl
from jax.experimental.pallas import tpu as pltpu
from jax.sharding import PartitionSpec as P

NH = 64
KVH = 8
HD = 128
GROUP = NH // KVH
PAIRS = KVH // 2
THETA = 500000.0
EPS = 1e-05
NEG = -1e30
MESH = pl.DeviceIdType.MESH
F32 = jnp.float32
BF16 = jnp.bfloat16


def three_parts(row):
    high = row.astype(BF16).astype(F32)
    rest = row - high
    middle = rest.astype(BF16).astype(F32)
    return [high, middle, rest - middle]


def layer_kernel(
    n,
    sections,
    lengths_ref,
    entering_ref,
    newcomer_ref,
    gain_hbm,
    query_hbm,
    keyvalue_hbm,
    keys_hbm,
    values_hbm,
    out_ref,
    query_w,
    keyvalue_w,
    keys,
    values,
    gain,
    inputs,
    normed,
    heads,
    fresh_heads,
    staged,
    parts,
    leaving,
    columns,
    load_sem,
    weight_sem,
    cache_sem,
    send_sem,
    recv_sem,
    heads_sem,
    ready_sem,
):
    ticks, rows, width = out_ref.shape
    features = query_w.shape[0]
    own_heads = NH // n
    own_rows = own_heads * rows
    kv_width = keyvalue_w.shape[1]
    pieces = HD // kv_width
    group_rows = GROUP * rows
    pair_rows = 2 * group_rows
    span = keys.shape[1] // rows
    chunks = weight_sem.shape[0]
    depth = features // chunks
    scale = 1.0 / math.sqrt(HD)

    section = lax.axis_index("section")
    me = lax.axis_index("kvp")

    gain_load = pltpu.make_async_copy(gain_hbm, gain, load_sem.at[0])
    gain_load.start()
    own_loads = [
        pltpu.make_async_copy(entering_ref, inputs.at[0, me], load_sem.at[1])
    ]
    own_loads[0].start()
    weight_loads = []
    for c in range(chunks):
        part = pl.ds(c * depth, depth)
        weight_loads.append(
            (
                pltpu.make_async_copy(query_hbm.at[part], query_w.at[part], weight_sem.at[c, 0]),
                pltpu.make_async_copy(
                    keyvalue_hbm.at[part], keyvalue_w.at[part], weight_sem.at[c, 1]
                ),
            )
        )
        for load in weight_loads[-1]:
            load.start()
    cache_loads = []
    for t in range(ticks):
        cache_loads.append(
            (
                pltpu.make_async_copy(keys_hbm.at[t], keys.at[t], cache_sem.at[t, 0]),
                pltpu.make_async_copy(values_hbm.at[t], values.at[t], cache_sem.at[t, 1]),
            )
        )
        for load in cache_loads[-1]:
            load.start()

    per_group = GROUP // own_heads
    own_group = me // per_group

    per_pair = 2 * per_group
    own_pair = me // per_pair

    def peer(step):
        pair = lax.rem(own_pair + step // per_pair, PAIRS)
        return pair * per_pair + lax.rem(me + step, per_pair)

    barrier = pltpu.get_barrier_semaphore()

    def greet(step, carry):
        pl.semaphore_signal(
            barrier, inc=1, device_id=(section, peer(step)), device_id_type=MESH
        )
        return carry

    lax.fori_loop(1, n, greet, 0)
    if sections > 1:

        @pl.when(section < sections - 1)
        def _():
            pl.semaphore_signal(barrier, inc=1, device_id=(section + 1, me), device_id_type=MESH)

        @pl.when(section > 0)
        def _():
            pl.semaphore_signal(barrier, inc=1, device_id=(section - 1, me), device_id_type=MESH)

    neighbours = (section > 0).astype(jnp.int32) + (section < sections - 1).astype(jnp.int32)
    pl.semaphore_wait(barrier, n - 1 + neighbours)
    if sections > 1:
        @pl.when(section > 0)
        def _():
            pl.semaphore_signal(ready_sem, inc=1, device_id=(section - 1, me), device_id_type=MESH)

    def spread(source, target, sent, received):
        def send(step, carry):
            pltpu.make_async_remote_copy(
                src_ref=source,
                dst_ref=target,
                send_sem=sent,
                recv_sem=received,
                device_id=(section, peer(step)),
                device_id_type=MESH,
            ).start()
            return carry

        lax.fori_loop(per_pair, n, send, 0)
        lax.fori_loop(1, per_pair, send, 0)

    def arrived(buffer, count, sem):
        whole = buffer.at[pl.ds(0, count)]
        pltpu.make_async_copy(whole, whole, sem).wait()

    spread(entering_ref, inputs.at[0, me], send_sem.at[0, 0], recv_sem.at[0, 0])

    @pl.when(section == 0)
    def _():
        for t in range(1, ticks):
            pltpu.make_async_copy(
                newcomer_ref.at[t - 1], inputs.at[t, me], load_sem.at[1 + t]
            ).start()
            spread(
                newcomer_ref.at[t - 1], inputs.at[t, me], send_sem.at[t, 0], recv_sem.at[t, 0]
            )

    lane = lax.broadcasted_iota(jnp.int32, (rows, HD), 1)
    row = lax.broadcasted_iota(jnp.int32, (rows, HD), 0)
    half = HD // 2
    exponent = (lane % half).astype(F32) * (2.0 / HD)
    frequency = jnp.exp(exponent * (-math.log(THETA)))
    turns = []
    masks = []
    place = lax.broadcasted_iota(jnp.int32, (rows * span, pair_rows), 0)
    column = lax.broadcasted_iota(jnp.int32, (rows * span, pair_rows), 1)
    position = me * span + place % span
    for t in range(ticks):
        micro = t + sections - 1 - section
        by_row = jnp.zeros((rows, HD), jnp.int32)
        limit = jnp.zeros((rows * span, pair_rows), jnp.int32)
        for b in range(rows):
            length = lengths_ref[micro, b]
            by_row = jnp.where(row == b, length, by_row)
            limit = jnp.where(column % rows == b, length, limit)
        angles = by_row.astype(F32) * frequency
        sine = jnp.sin(angles)
        turns.append((jnp.cos(angles), jnp.where(lane < half, -sine, sine)))
        masks.append((place // span == column % rows) & (position < limit))

    def rotated(head, t):
        cosine, sine = turns[t]
        return head * cosine + pltpu.roll(head, half, 1) * sine

    kinds = n // 2
    fresh_group = (me % kinds) // pieces
    fresh_slot = (me // kinds) * pieces + me % pieces
    at_home = fresh_group == own_group

    def fresh_all(tick, sem, count):
        @pl.when(at_home)
        def _():
            if count > 1:
                arrived(fresh_heads.at[tick], count - 1, sem)

        @pl.when(jnp.logical_not(at_home))
        def _():
            arrived(fresh_heads.at[tick], count, sem)

    gain_load.wait()
    for t in range(ticks):
        if t == 0:
            own_loads[0].wait()
            arrived(inputs.at[0], n - 1, recv_sem.at[0, 0])
        else:

            @pl.when(section == 0)
            def _():
                pltpu.make_async_copy(
                    newcomer_ref.at[t - 1], inputs.at[t, me], load_sem.at[1 + t]
                ).wait()
                arrived(inputs.at[t], n - 1, recv_sem.at[t, 0])

            @pl.when(section > 0)
            def _():
                arrived(inputs.at[t], n, recv_sem.at[t, 0])

        squares = jnp.zeros((rows, width), F32)
        for s in range(n):
            x = inputs[t, s].astype(F32)
            squares = squares + x * x
        mean_square = jnp.sum(squares, axis=-1, keepdims=True) * (1.0 / features)
        factor = lax.rsqrt(mean_square + EPS)
        for s in range(n):
            part = pl.ds(s * width, width)
            x = inputs[t, s].astype(F32)
            normed[:, part] = (x * factor * gain[:, part].astype(F32)).astype(BF16)

        query = jnp.zeros((rows, width), F32)
        for c in range(chunks):
            part = pl.ds(c * depth, depth)
            if t == 0:
                weight_loads[c][0].wait()
            query = query + jnp.dot(normed[:, part], query_w[part], preferred_element_type=F32)
        heads[t, me] = jnp.concatenate(
            [rotated(query[:, h * HD : (h + 1) * HD], t) for h in range(own_heads)], axis=0
        ).astype(BF16)
        spread(heads.at[t, me], heads.at[t, me], send_sem.at[t, 1], heads_sem.at[t, own_pair])
        fresh = jnp.zeros((rows, kv_width), F32)
        for c in range(chunks):
            part = pl.ds(c * depth, depth)
            if t == 0:
                weight_loads[c][1].wait()
            fresh = fresh + jnp.dot(normed[:, part], keyvalue_w[part], preferred_element_type=F32)
        fresh = fresh.astype(BF16)
        if pieces > 1:
            fresh = jnp.concatenate([fresh.astype(F32)] * pieces, axis=1)
            fresh = jnp.where(lane // kv_width == me % pieces, fresh, 0.0).astype(BF16)
        fresh_heads[t, 2 * pieces] = fresh
        for j in range(per_group):
            target = fresh_group * per_group + j

            @pl.when(target == me)
            def _():
                fresh_heads[t, fresh_slot] = fresh

            @pl.when(target != me)
            def _():
                pltpu.make_async_remote_copy(
                    src_ref=fresh_heads.at[t, 2 * pieces],
                    dst_ref=fresh_heads.at[t, fresh_slot],
                    send_sem=send_sem.at[t, 4],
                    recv_sem=recv_sem.at[t, 1],
                    device_id=(section, target),
                    device_id_type=MESH,
                ).start()

        for load in cache_loads[t]:
            load.wait()
        valid = masks[t]
        upper = lax.broadcasted_iota(jnp.int32, (pair_rows, HD), 0) < group_rows
        for k in [*range(1, PAIRS), 0]:
            pair = lax.rem(own_pair + PAIRS - k, PAIRS)
            arrived(heads.at[t], per_pair - (k == 0), heads_sem.at[t, pair])
            both = jnp.concatenate(
                [heads[t, pair * per_pair + j].astype(F32) for j in range(per_pair)], axis=0
            )
            both = jnp.concatenate(
                [jnp.where(upper, both, 0.0), jnp.where(upper, 0.0, both)], axis=1
            ).astype(BF16)
            part = pl.ds(pl.multiple_of(pair * 2 * HD, 2 * HD), 2 * HD)
            scores = lax.dot_general(
                keys[t, :, part],
                both,
                (((1,), (1,)), ((), ())),
                preferred_element_type=F32,
            )
            scores = jnp.where(valid, scores * scale, NEG)
            top = jnp.max(scores, axis=0, keepdims=True)
            weights = jnp.where(valid, jnp.exp(scores - top), 0.0)
            total = jnp.sum(weights, axis=0, keepdims=True)
            weighted = lax.dot_general(
                weights.astype(BF16),
                values[t, :, part],
                (((0,), (0,)), ((), ())),
                preferred_element_type=F32,
            )
            weighted = jnp.where(upper, weighted[:, :HD], weighted[:, HD:])
            stats = jnp.concatenate(
                three_parts(top) + three_parts(total) + [jnp.zeros((2, pair_rows), F32)], axis=0
            )
            for j in range(per_pair):
                target = pair * per_pair + j
                message = jnp.concatenate(
                    [weighted[j * own_rows : (j + 1) * own_rows], stats], axis=0
                ).astype(BF16)
                staged[t, target] = message

                def send():
                    pltpu.make_async_remote_copy(
                        src_ref=staged.at[t, target],
                        dst_ref=parts.at[t, me],
                        send_sem=send_sem.at[t, 2],
                        recv_sem=recv_sem.at[t, 2],
                        device_id=(section, target),
                        device_id_type=MESH,
                    ).start()

                if k > 0:
                    send()
                else:

                    @pl.when(target == me)
                    def _():
                        parts[t, me] = message

                    pl.when(target != me)(send)

        fresh_all(t, recv_sem.at[t, 1], 2 * pieces)
        new_key = jnp.zeros((rows, HD), F32)
        new_value = jnp.zeros((rows, HD), F32)
        for j in range(pieces):
            new_key = new_key + fresh_heads[t, j].astype(F32)
            new_value = new_value + fresh_heads[t, pieces + j].astype(F32)
        new_key = jnp.concatenate([rotated(new_key, t)] * own_heads, axis=0)
        new_value = jnp.concatenate([new_value] * own_heads, axis=0)
        own_query = heads[t, me].astype(F32)
        new_score = jnp.sum(own_query * new_key, axis=-1, keepdims=True) * scale

        arrived(parts.at[t], n - 1, recv_sem.at[t, 2])
        tops = []
        totals = []
        for s in range(n):
            stats = parts[t, s].astype(F32)[own_rows : own_rows + 8]
            tops.append(stats[0:1] + stats[1:2] + stats[2:3])
            totals.append(stats[3:4] + stats[4:5] + stats[5:6])
        blank = HD - n
        tops = jnp.concatenate(tops + [jnp.full((blank, HD), NEG, F32)], axis=0)
        totals = jnp.concatenate(totals + [jnp.zeros((blank, HD), F32)], axis=0)
        columns[0] = tops.T
        columns[1] = totals.T
        first = pl.multiple_of((me % per_pair) * own_rows, 8)
        tops = columns[0, pl.ds(first, own_rows), :]
        totals = columns[1, pl.ds(first, own_rows), :]
        top = jnp.maximum(jnp.max(tops, axis=-1, keepdims=True), new_score)
        factors = jnp.exp(tops - top)
        new_weight = jnp.exp(new_score - top)
        denominator = jnp.sum(factors * totals, axis=-1, keepdims=True) + new_weight
        numerator = new_weight * new_value
        for s in range(n):
            part = parts[t, s].astype(F32)[:own_rows]
            numerator = numerator + part * factors[:, s : s + 1]
        attended = numerator / denominator
        attended = jnp.concatenate(
            [attended[h * rows : (h + 1) * rows] for h in range(own_heads)], axis=1
        )
        result = (inputs[t, me].astype(F32) + attended).astype(BF16)
        out_ref[t] = result
        if t < ticks - 1 and sections > 1:
            leaving[t] = result

            @pl.when(section < sections - 1)
            def _():
                if t == 0:
                    pl.semaphore_wait(ready_sem, 1)

                def send(step, carry):
                    pltpu.make_async_remote_copy(
                        src_ref=leaving.at[t],
                        dst_ref=inputs.at[t + 1, me],
                        send_sem=send_sem.at[t, 3],
                        recv_sem=recv_sem.at[t + 1, 0],
                        device_id=(section + 1, peer(step)),
                        device_id_type=MESH,
                    ).start()
                    return carry

                lax.fori_loop(0, n, send, 0)

    for t in range(ticks):
        if t == 0:
            arrived(inputs.at[t], n - 1, send_sem.at[t, 0])
        else:

            @pl.when(section == 0)
            def _():
                arrived(inputs.at[t], n - 1, send_sem.at[t, 0])

        arrived(heads.at[t], n - 1, send_sem.at[t, 1])
        fresh_all(t, send_sem.at[t, 4], per_group)
        arrived(parts.at[t], n - 1, send_sem.at[t, 2])
        if t < ticks - 1 and sections > 1:

            @pl.when(section < sections - 1)
            def _():
                arrived(inputs.at[t], n, send_sem.at[t, 3])


def shards(
    n,
    sections,
    entering,
    newcomer,
    norm_gain,
    query_weight,
    keyvalue_weight,
    key_cache,
    value_cache,
    cache_lengths,
):
    _, rows, width = entering.shape
    _, features, _ = query_weight.shape
    kv_width = keyvalue_weight.shape[2]
    _, ticks, _, span, kv_features = key_cache.shape
    own_rows = (NH // n) * rows
    message_rows = own_rows + 8
    pieces = HD // kv_width
    slots = max(2 * pieces + 1, NH // KVH * n // NH)
    chunks = 4
    anywhere = pl.BlockSpec(memory_space=pl.ANY)
    out = pl.pallas_call(
        functools.partial(layer_kernel, n, sections),
        out_shape=jax.ShapeDtypeStruct((ticks, rows, width), BF16),
        in_specs=[pl.BlockSpec(memory_space=pltpu.SMEM)] + [anywhere] * 7,
        out_specs=pl.BlockSpec(memory_space=pltpu.VMEM),
        scratch_shapes=[
            pltpu.VMEM((features, width), BF16),
            pltpu.VMEM((features, kv_width), BF16),
            pltpu.VMEM((ticks, rows * span, kv_features), BF16),
            pltpu.VMEM((ticks, rows * span, kv_features), BF16),
            pltpu.VMEM((1, features), BF16),
            pltpu.VMEM((ticks, n, rows, width), BF16),
            pltpu.VMEM((rows, features), BF16),
            pltpu.VMEM((ticks, n, own_rows, HD), BF16),
            pltpu.VMEM((ticks, slots, rows, HD), BF16),
            pltpu.VMEM((ticks, n, message_rows, HD), BF16),
            pltpu.VMEM((ticks, n, message_rows, HD), BF16),
            pltpu.VMEM((ticks, rows, width), BF16),
            pltpu.VMEM((2, HD, HD), F32),
            pltpu.SemaphoreType.DMA((1 + ticks,)),
            pltpu.SemaphoreType.DMA((chunks, 2)),
            pltpu.SemaphoreType.DMA((ticks, 2)),
            pltpu.SemaphoreType.DMA((ticks, 5)),
            pltpu.SemaphoreType.DMA((ticks, 3)),
            pltpu.SemaphoreType.DMA((ticks, PAIRS)),
            pltpu.SemaphoreType.REGULAR,
        ],
        compiler_params=pltpu.CompilerParams(
            collective_id=0, has_side_effects=True, vmem_limit_bytes=60 << 20
        ),
    )(
        cache_lengths,
        entering[0],
        newcomer,
        norm_gain,
        query_weight[0],
        keyvalue_weight[0],
        key_cache.reshape(ticks, rows * span, kv_features),
        value_cache.reshape(ticks, rows * span, kv_features),
    )
    return out[None]


def solution(mesh):
    placed = (
        P("section", None, "kvp"),
        P(None, None, "kvp"),
        P("section", None),
        P("section", None, "kvp"),
        P("section", None, "kvp"),
        P("section", None, None, "kvp", None),
        P("section", None, None, "kvp", None),
        P(),
    )
    return jax.shard_map(
        functools.partial(shards, mesh.shape["kvp"], mesh.shape["section"]),
        mesh=mesh,
        in_specs=placed,
        out_specs=P("section", None, None, "kvp"),
        check_vma=False,
    )
```

```python
import functools
import math

import jax
import jax.numpy as jnp
from jax import lax
from jax.experimental import pallas as pl
from jax.experimental.pallas import tpu as pltpu
from jax.sharding import PartitionSpec as P

NH = 64
KVH = 8
HD = 128
GROUP = NH // KVH
PAIRS = KVH // 2
THETA = 500000.0
EPS = 1e-05
NEG = -1e30
MESH = pl.DeviceIdType.MESH
F32 = jnp.float32
BF16 = jnp.bfloat16


def three_parts(row):
    high = row.astype(BF16).astype(F32)
    rest = row - high
    middle = rest.astype(BF16).astype(F32)
    return [high, middle, rest - middle]


def layer_kernel(
    n,
    sections,
    lengths_ref,
    entering_ref,
    newcomer_ref,
    gain_hbm,
    query_hbm,
    keyvalue_hbm,
    keys_hbm,
    values_hbm,
    out_ref,
    query_w,
    keyvalue_w,
    keys,
    values,
    gain,
    inputs,
    normed,
    heads,
    fresh_heads,
    staged,
    parts,
    leaving,
    columns,
    load_sem,
    weight_sem,
    cache_sem,
    send_sem,
    recv_sem,
    heads_sem,
    ready_sem,
):
    ticks, rows, width = out_ref.shape
    features = query_w.shape[0]
    own_heads = NH // n
    own_rows = own_heads * rows
    kv_width = keyvalue_w.shape[1]
    pieces = HD // kv_width
    group_rows = GROUP * rows
    pair_rows = 2 * group_rows
    span = keys.shape[1] // rows
    chunks = weight_sem.shape[0]
    depth = features // chunks
    scale = 1.0 / math.sqrt(HD)

    section = lax.axis_index("section")
    me = lax.axis_index("kvp")

    gain_load = pltpu.make_async_copy(gain_hbm, gain, load_sem.at[0])
    gain_load.start()
    own_loads = [
        pltpu.make_async_copy(entering_ref, inputs.at[0, me], load_sem.at[1])
    ]
    own_loads[0].start()
    weight_loads = []
    for c in range(chunks):
        part = pl.ds(c * depth, depth)
        weight_loads.append(
            (
                pltpu.make_async_copy(query_hbm.at[part], query_w.at[part], weight_sem.at[c, 0]),
                pltpu.make_async_copy(
                    keyvalue_hbm.at[part], keyvalue_w.at[part], weight_sem.at[c, 1]
                ),
            )
        )
        for load in weight_loads[-1]:
            load.start()
    cache_loads = []
    for t in range(ticks):
        cache_loads.append(
            (
                pltpu.make_async_copy(keys_hbm.at[t], keys.at[t], cache_sem.at[t, 0]),
                pltpu.make_async_copy(values_hbm.at[t], values.at[t], cache_sem.at[t, 1]),
            )
        )
        for load in cache_loads[-1]:
            load.start()

    per_group = GROUP // own_heads
    own_group = me // per_group

    per_pair = 2 * per_group
    own_pair = me // per_pair

    def peer(step):
        pair = lax.rem(own_pair + step // per_pair, PAIRS)
        return pair * per_pair + lax.rem(me + step, per_pair)

    barrier = pltpu.get_barrier_semaphore()

    def greet(step, carry):
        pl.semaphore_signal(
            barrier, inc=1, device_id=(section, peer(step)), device_id_type=MESH
        )
        return carry

    lax.fori_loop(1, n, greet, 0)
    if sections > 1:

        @pl.when(section < sections - 1)
        def _():
            pl.semaphore_signal(barrier, inc=1, device_id=(section + 1, me), device_id_type=MESH)

        @pl.when(section > 0)
        def _():
            pl.semaphore_signal(barrier, inc=1, device_id=(section - 1, me), device_id_type=MESH)

    neighbours = (section > 0).astype(jnp.int32) + (section < sections - 1).astype(jnp.int32)
    pl.semaphore_wait(barrier, n - 1 + neighbours)
    if sections > 1:
        @pl.when(section > 0)
        def _():
            pl.semaphore_signal(ready_sem, inc=1, device_id=(section - 1, me), device_id_type=MESH)

    def spread(source, target, sent, received):
        def send(step, carry):
            pltpu.make_async_remote_copy(
                src_ref=source,
                dst_ref=target,
                send_sem=sent,
                recv_sem=received,
                device_id=(section, peer(step)),
                device_id_type=MESH,
            ).start()
            return carry

        lax.fori_loop(1, n, send, 0)

    def arrived(buffer, count, sem):
        whole = buffer.at[pl.ds(0, count)]
        pltpu.make_async_copy(whole, whole, sem).wait()

    spread(entering_ref, inputs.at[0, me], send_sem.at[0, 0], recv_sem.at[0, 0])

    @pl.when(section == 0)
    def _():
        for t in range(1, ticks):
            pltpu.make_async_copy(
                newcomer_ref.at[t - 1], inputs.at[t, me], load_sem.at[1 + t]
            ).start()

    lane = lax.broadcasted_iota(jnp.int32, (rows, HD), 1)
    row = lax.broadcasted_iota(jnp.int32, (rows, HD), 0)
    half = HD // 2
    exponent = (lane % half).astype(F32) * (2.0 / HD)
    frequency = jnp.exp(exponent * (-math.log(THETA)))
    turns = []
    masks = []
    place = lax.broadcasted_iota(jnp.int32, (rows * span, pair_rows), 0)
    column = lax.broadcasted_iota(jnp.int32, (rows * span, pair_rows), 1)
    position = me * span + place % span
    for t in range(ticks):
        micro = t + sections - 1 - section
        by_row = jnp.zeros((rows, HD), jnp.int32)
        limit = jnp.zeros((rows * span, pair_rows), jnp.int32)
        for b in range(rows):
            length = lengths_ref[micro, b]
            by_row = jnp.where(row == b, length, by_row)
            limit = jnp.where(column % rows == b, length, limit)
        angles = by_row.astype(F32) * frequency
        sine = jnp.sin(angles)
        turns.append((jnp.cos(angles), jnp.where(lane < half, -sine, sine)))
        masks.append((place // span == column % rows) & (position < limit))

    def rotated(head, t):
        cosine, sine = turns[t]
        return head * cosine + pltpu.roll(head, half, 1) * sine

    kinds = n // 2
    fresh_group = (me % kinds) // pieces
    fresh_slot = (me // kinds) * pieces + me % pieces
    at_home = fresh_group == own_group

    def fresh_all(tick, sem, count):
        @pl.when(at_home)
        def _():
            if count > 1:
                arrived(fresh_heads.at[tick], count - 1, sem)

        @pl.when(jnp.logical_not(at_home))
        def _():
            arrived(fresh_heads.at[tick], count, sem)

    gain_load.wait()
    for t in range(ticks):
        if t == 0:
            own_loads[0].wait()
            arrived(inputs.at[0], n - 1, recv_sem.at[0, 0])
        else:

            @pl.when(section == 0)
            def _():
                pltpu.make_async_copy(
                    newcomer_ref.at[t - 1], inputs.at[t, me], load_sem.at[1 + t]
                ).wait()
                arrived(inputs.at[t], n - 1, recv_sem.at[t, 0])

            @pl.when(section > 0)
            def _():
                arrived(inputs.at[t], n, recv_sem.at[t, 0])

        squares = jnp.zeros((rows, width), F32)
        for s in range(n):
            x = inputs[t, s].astype(F32)
            squares = squares + x * x
        mean_square = jnp.sum(squares, axis=-1, keepdims=True) * (1.0 / features)
        factor = lax.rsqrt(mean_square + EPS)
        for s in range(n):
            part = pl.ds(s * width, width)
            x = inputs[t, s].astype(F32)
            normed[:, part] = (x * factor * gain[:, part].astype(F32)).astype(BF16)

        query = jnp.zeros((rows, width), F32)
        for c in range(chunks):
            part = pl.ds(c * depth, depth)
            if t == 0:
                weight_loads[c][0].wait()
            query = query + jnp.dot(normed[:, part], query_w[part], preferred_element_type=F32)
        heads[t, me] = jnp.concatenate(
            [rotated(query[:, h * HD : (h + 1) * HD], t) for h in range(own_heads)], axis=0
        ).astype(BF16)
        spread(heads.at[t, me], heads.at[t, me], send_sem.at[t, 1], heads_sem.at[t, own_pair])
        fresh = jnp.zeros((rows, kv_width), F32)
        for c in range(chunks):
            part = pl.ds(c * depth, depth)
            if t == 0:
                weight_loads[c][1].wait()
            fresh = fresh + jnp.dot(normed[:, part], keyvalue_w[part], preferred_element_type=F32)
        fresh = fresh.astype(BF16)
        if pieces > 1:
            fresh = jnp.concatenate([fresh.astype(F32)] * pieces, axis=1)
            fresh = jnp.where(lane // kv_width == me % pieces, fresh, 0.0).astype(BF16)
        fresh_heads[t, 2 * pieces] = fresh
        for j in range(per_group):
            target = fresh_group * per_group + j

            @pl.when(target == me)
            def _():
                fresh_heads[t, fresh_slot] = fresh

            @pl.when(target != me)
            def _():
                pltpu.make_async_remote_copy(
                    src_ref=fresh_heads.at[t, 2 * pieces],
                    dst_ref=fresh_heads.at[t, fresh_slot],
                    send_sem=send_sem.at[t, 4],
                    recv_sem=recv_sem.at[t, 1],
                    device_id=(section, target),
                    device_id_type=MESH,
                ).start()

        for load in cache_loads[t]:
            load.wait()
        valid = masks[t]
        upper = lax.broadcasted_iota(jnp.int32, (pair_rows, HD), 0) < group_rows
        for k in range(PAIRS):
            pair = lax.rem(own_pair + PAIRS - k, PAIRS)
            arrived(heads.at[t], per_pair - (k == 0), heads_sem.at[t, pair])
            both = jnp.concatenate(
                [heads[t, pair * per_pair + j].astype(F32) for j in range(per_pair)], axis=0
            )
            both = jnp.concatenate(
                [jnp.where(upper, both, 0.0), jnp.where(upper, 0.0, both)], axis=1
            ).astype(BF16)
            part = pl.ds(pl.multiple_of(pair * 2 * HD, 2 * HD), 2 * HD)
            scores = lax.dot_general(
                keys[t, :, part],
                both,
                (((1,), (1,)), ((), ())),
                preferred_element_type=F32,
            )
            scores = jnp.where(valid, scores * scale, NEG)
            top = jnp.max(scores, axis=0, keepdims=True)
            weights = jnp.where(valid, jnp.exp(scores - top), 0.0)
            total = jnp.sum(weights, axis=0, keepdims=True)
            weighted = lax.dot_general(
                weights.astype(BF16),
                values[t, :, part],
                (((0,), (0,)), ((), ())),
                preferred_element_type=F32,
            )
            weighted = jnp.where(upper, weighted[:, :HD], weighted[:, HD:])
            stats = jnp.concatenate(
                three_parts(top) + three_parts(total) + [jnp.zeros((2, pair_rows), F32)], axis=0
            )
            for j in range(per_pair):
                target = pair * per_pair + j
                message = jnp.concatenate(
                    [weighted[j * own_rows : (j + 1) * own_rows], stats], axis=0
                ).astype(BF16)
                staged[t, target] = message

                def send():
                    pltpu.make_async_remote_copy(
                        src_ref=staged.at[t, target],
                        dst_ref=parts.at[t, me],
                        send_sem=send_sem.at[t, 2],
                        recv_sem=recv_sem.at[t, 2],
                        device_id=(section, target),
                        device_id_type=MESH,
                    ).start()

                if k > 0:
                    send()
                else:

                    @pl.when(target == me)
                    def _():
                        parts[t, me] = message

                    pl.when(target != me)(send)

        fresh_all(t, recv_sem.at[t, 1], 2 * pieces)
        new_key = jnp.zeros((rows, HD), F32)
        new_value = jnp.zeros((rows, HD), F32)
        for j in range(pieces):
            new_key = new_key + fresh_heads[t, j].astype(F32)
            new_value = new_value + fresh_heads[t, pieces + j].astype(F32)
        new_key = jnp.concatenate([rotated(new_key, t)] * own_heads, axis=0)
        new_value = jnp.concatenate([new_value] * own_heads, axis=0)
        own_query = heads[t, me].astype(F32)
        new_score = jnp.sum(own_query * new_key, axis=-1, keepdims=True) * scale

        arrived(parts.at[t], n - 1, recv_sem.at[t, 2])
        if t < ticks - 1:
            @pl.when(section == 0)
            def _():
                spread(
                    newcomer_ref.at[t],
                    inputs.at[t + 1, me],
                    send_sem.at[t + 1, 0],
                    recv_sem.at[t + 1, 0],
                )

        tops = []
        totals = []
        for s in range(n):
            stats = parts[t, s].astype(F32)[own_rows : own_rows + 8]
            tops.append(stats[0:1] + stats[1:2] + stats[2:3])
            totals.append(stats[3:4] + stats[4:5] + stats[5:6])
        blank = HD - n
        tops = jnp.concatenate(tops + [jnp.full((blank, HD), NEG, F32)], axis=0)
        totals = jnp.concatenate(totals + [jnp.zeros((blank, HD), F32)], axis=0)
        columns[0] = tops.T
        columns[1] = totals.T
        first = pl.multiple_of((me % per_pair) * own_rows, 8)
        tops = columns[0, pl.ds(first, own_rows), :]
        totals = columns[1, pl.ds(first, own_rows), :]
        top = jnp.maximum(jnp.max(tops, axis=-1, keepdims=True), new_score)
        factors = jnp.exp(tops - top)
        new_weight = jnp.exp(new_score - top)
        denominator = jnp.sum(factors * totals, axis=-1, keepdims=True) + new_weight
        numerator = new_weight * new_value
        for s in range(n):
            part = parts[t, s].astype(F32)[:own_rows]
            numerator = numerator + part * factors[:, s : s + 1]
        attended = numerator / denominator
        attended = jnp.concatenate(
            [attended[h * rows : (h + 1) * rows] for h in range(own_heads)], axis=1
        )
        result = (inputs[t, me].astype(F32) + attended).astype(BF16)
        out_ref[t] = result
        if t < ticks - 1 and sections > 1:
            leaving[t] = result

            @pl.when(section < sections - 1)
            def _():
                if t == 0:
                    pl.semaphore_wait(ready_sem, 1)

                def send(step, carry):
                    pltpu.make_async_remote_copy(
                        src_ref=leaving.at[t],
                        dst_ref=inputs.at[t + 1, me],
                        send_sem=send_sem.at[t, 3],
                        recv_sem=recv_sem.at[t + 1, 0],
                        device_id=(section + 1, peer(step)),
                        device_id_type=MESH,
                    ).start()
                    return carry

                lax.fori_loop(0, n, send, 0)

    for t in range(ticks):
        if t == 0:
            arrived(inputs.at[t], n - 1, send_sem.at[t, 0])
        else:

            @pl.when(section == 0)
            def _():
                arrived(inputs.at[t], n - 1, send_sem.at[t, 0])

        arrived(heads.at[t], n - 1, send_sem.at[t, 1])
        fresh_all(t, send_sem.at[t, 4], per_group)
        arrived(parts.at[t], n - 1, send_sem.at[t, 2])
        if t < ticks - 1 and sections > 1:

            @pl.when(section < sections - 1)
            def _():
                arrived(inputs.at[t], n, send_sem.at[t, 3])


def shards(
    n,
    sections,
    entering,
    newcomer,
    norm_gain,
    query_weight,
    keyvalue_weight,
    key_cache,
    value_cache,
    cache_lengths,
):
    _, rows, width = entering.shape
    _, features, _ = query_weight.shape
    kv_width = keyvalue_weight.shape[2]
    _, ticks, _, span, kv_features = key_cache.shape
    own_rows = (NH // n) * rows
    message_rows = own_rows + 8
    pieces = HD // kv_width
    slots = max(2 * pieces + 1, NH // KVH * n // NH)
    chunks = 4
    anywhere = pl.BlockSpec(memory_space=pl.ANY)
    out = pl.pallas_call(
        functools.partial(layer_kernel, n, sections),
        out_shape=jax.ShapeDtypeStruct((ticks, rows, width), BF16),
        in_specs=[pl.BlockSpec(memory_space=pltpu.SMEM)] + [anywhere] * 7,
        out_specs=pl.BlockSpec(memory_space=pltpu.VMEM),
        scratch_shapes=[
            pltpu.VMEM((features, width), BF16),
            pltpu.VMEM((features, kv_width), BF16),
            pltpu.VMEM((ticks, rows * span, kv_features), BF16),
            pltpu.VMEM((ticks, rows * span, kv_features), BF16),
            pltpu.VMEM((1, features), BF16),
            pltpu.VMEM((ticks, n, rows, width), BF16),
            pltpu.VMEM((rows, features), BF16),
            pltpu.VMEM((ticks, n, own_rows, HD), BF16),
            pltpu.VMEM((ticks, slots, rows, HD), BF16),
            pltpu.VMEM((ticks, n, message_rows, HD), BF16),
            pltpu.VMEM((ticks, n, message_rows, HD), BF16),
            pltpu.VMEM((ticks, rows, width), BF16),
            pltpu.VMEM((2, HD, HD), F32),
            pltpu.SemaphoreType.DMA((1 + ticks,)),
            pltpu.SemaphoreType.DMA((chunks, 2)),
            pltpu.SemaphoreType.DMA((ticks, 2)),
            pltpu.SemaphoreType.DMA((ticks, 5)),
            pltpu.SemaphoreType.DMA((ticks, 3)),
            pltpu.SemaphoreType.DMA((ticks, PAIRS)),
            pltpu.SemaphoreType.REGULAR,
        ],
        compiler_params=pltpu.CompilerParams(
            collective_id=0, has_side_effects=True, vmem_limit_bytes=60 << 20
        ),
    )(
        cache_lengths,
        entering[0],
        newcomer,
        norm_gain,
        query_weight[0],
        keyvalue_weight[0],
        key_cache.reshape(ticks, rows * span, kv_features),
        value_cache.reshape(ticks, rows * span, kv_features),
    )
    return out[None]


def solution(mesh):
    placed = (
        P("section", None, "kvp"),
        P(None, None, "kvp"),
        P("section", None),
        P("section", None, "kvp"),
        P("section", None, "kvp"),
        P("section", None, None, "kvp", None),
        P("section", None, None, "kvp", None),
        P(),
    )
    return jax.shard_map(
        functools.partial(shards, mesh.shape["kvp"], mesh.shape["section"]),
        mesh=mesh,
        in_specs=placed,
        out_specs=P("section", None, None, "kvp"),
        check_vma=False,
    )
```
